32 devices in a mesh: ctx: 8 (over z, x), head: 4 (over y, core).
Axes of the slice: x: 2, y: 2, z: 4, core: 2. Of those that a mesh axis runs over, the one named last changes fastest.
Arguments:
- positions: int32 [128], replicated, may hold values from 1 to 8191, as said below
- mla_queries: bfloat16 [128, 128, 576], P(None, 'head'), may hold values from -5000 to 5000
- latent_keys: bfloat16 [8192, 576], P('ctx'), may hold values from -18 to 18
- index_queries: bfloat16 [128, 64, 128], P(None, 'head'), may hold values from -64 to 64
- index_keys: bfloat16 [8192, 128], P('ctx'), may hold values from -18 to 18
- head_weights: float32 [128, 64], P(None, 'head'), may hold values from -4 to 4
Outputs:
- grad_queries: float32 [128, 64, 128], P('ctx', 'head')
- grad_keys: float32 [8192, 128], P(('ctx', 'head'))
- grad_weights: float32 [128, 64], P('ctx', 'head')
The draws below stay inside these ranges and needn't reach their ends.
Inputs may be any that keep to these rules, and one draw needn't show every extreme that they name: Each query sees the keys at positions 0 to its own position.
All inputs are finite; a program needn't handle non-finite values.
Results may differ from the reference program's by a relative error of at most 0.0045.
Values may be sent and summed in bfloat16 or wider, within the bound.
A program may use at most 128 MiB of HBM per device.

```python
import math
import jax
import jax.numpy as jnp
from jax import lax

HEADS = 128
DQK = 576
QK_HEAD = 192
HI = 64
DI = 128
Q = 128
KEYS = 8192


def draw_tables(key):
    streams = jax.random.split(jax.random.fold_in(key, 7), 7)
    positions = jax.random.randint(streams[0], (Q,), 1, KEYS, dtype=jnp.int32)
    query_scale = 1.5 * math.sqrt(QK_HEAD / DQK)
    weight_scale = 2.0 * math.sqrt(2.0 / HI)
    latent = jnp.clip(jax.random.normal(streams[2], (KEYS, DQK), jnp.float32), -6.0, 6.0)
    index = jnp.clip(jax.random.normal(streams[3], (KEYS, DI), jnp.float32), -6.0, 6.0)
    mla = jnp.clip(jax.random.normal(streams[4], (Q, HEADS, DQK), jnp.float32), -6.0, 6.0) * query_scale
    index_query = jnp.clip(jax.random.normal(streams[5], (Q, HI, DI), jnp.float32), -6.0, 6.0) / math.sqrt(DI)
    weights = jnp.clip(jax.random.normal(streams[6], (Q, HI), jnp.float32), -6.0, 6.0) * weight_scale
    mla = jnp.clip(mla, -5000.0, 5000.0)
    index_query = jnp.clip(index_query, -64.0, 64.0)
    return (positions, mla, latent, index_query, index, weights)


def draw_positions(key, part):
    return draw_tables(key)[0]


def draw_mla_queries(key, part):
    return draw_tables(key)[1].astype(jnp.bfloat16)


def draw_latent_keys(key, part):
    return draw_tables(key)[2].astype(jnp.bfloat16)


def draw_index_queries(key, part):
    return draw_tables(key)[3].astype(jnp.bfloat16)


def draw_index_keys(key, part):
    return draw_tables(key)[4].astype(jnp.bfloat16)


def draw_head_weights(key, part):
    return draw_tables(key)[5]


def setup_inputs(seed: int = 0) -> dict:
    key_list = jax.random.split(jax.random.key(seed), 7)
    positions = draw_positions(jax.random.fold_in(key_list[6], 71), 0)
    mla_queries = draw_mla_queries(jax.random.fold_in(key_list[6], 71), 0)
    latent_keys = draw_latent_keys(jax.random.fold_in(key_list[6], 71), 0)
    index_queries = draw_index_queries(jax.random.fold_in(key_list[6], 71), 0)
    index_keys = draw_index_keys(jax.random.fold_in(key_list[6], 71), 0)
    head_weights = draw_head_weights(jax.random.fold_in(key_list[6], 71), 0)
    return dict(positions=positions, mla_queries=mla_queries, latent_keys=latent_keys, index_queries=index_queries, index_keys=index_keys, head_weights=head_weights)


masked_value = -1e+30

def reference(positions, mla_queries, latent_keys, index_queries, index_keys, head_weights):
    keys_total = latent_keys.shape[0]
    key_pos = jnp.arange(keys_total, dtype=jnp.int32)
    allowed = key_pos[None, :] <= positions[:, None]
    score_scale = 1.0 / math.sqrt(QK_HEAD)

    def softmax_rows(values):
        highest = lax.optimization_barrier(jnp.max(jnp.where(allowed, values, masked_value), axis=1, keepdims=True))
        exponent = jnp.where(allowed, jnp.exp(values - highest), 0.0)
        return exponent / lax.optimization_barrier(jnp.sum(exponent, axis=1, keepdims=True))

    def add_head(total, query):
        scores = jnp.dot(query, latent_keys.T, preferred_element_type=jnp.float32) * score_scale
        return (total + softmax_rows(scores), None)
    start_zero = jnp.zeros((positions.shape[0], keys_total), jnp.float32)
    target, _ = lax.scan(add_head, start_zero, jnp.swapaxes(mla_queries, 0, 1))
    target = target / HEADS

    def add_logits(total, pair):
        query, weight = pair
        inner = jnp.dot(query, index_keys.T, preferred_element_type=jnp.float32)
        return (total + weight[:, None] * jnp.maximum(inner, 0.0), None)
    head_queries = jnp.swapaxes(index_queries, 0, 1)
    logits, _ = lax.scan(add_logits, start_zero, (head_queries, head_weights.T))
    predicted = softmax_rows(logits)
    gradient = jnp.where(allowed, math.sqrt(keys_total) * (predicted - target), 0.0).astype(jnp.bfloat16)
    grad_float = gradient.astype(jnp.float32)

    def head_grads(carry, pair):
        query, weight = pair
        inner = jnp.dot(query, index_keys.T, preferred_element_type=jnp.float32)
        active = jnp.maximum(inner, 0.0)
        weight_grad = lax.optimization_barrier(jnp.sum(grad_float * active, axis=1))
        delta = jnp.where(inner > 0, grad_float * weight[:, None], 0.0).astype(jnp.bfloat16)
        query_grad = jnp.dot(delta, index_keys, preferred_element_type=jnp.float32)
        carry = carry + jnp.dot(delta.T, query, preferred_element_type=jnp.float32)
        return (carry, (query_grad, weight_grad))
    key_zero = jnp.zeros((keys_total, index_keys.shape[1]), jnp.float32)
    grad_keys, (query_grads, weight_grads) = lax.scan(head_grads, key_zero, (head_queries, head_weights.T))
    return (jnp.swapaxes(query_grads, 0, 1), grad_keys, weight_grads.T)
```

```python
import functools
import math

import jax
import jax.numpy as jnp
from jax import lax
from jax.experimental import pallas as pl
from jax.experimental.pallas import tpu as pltpu
from jax.sharding import PartitionSpec as P

HEADS = 128
QK_HEAD = 192
LANES = 256
GROUP = 4
MESH = pl.DeviceIdType.MESH
F32 = jnp.float32
BF16 = jnp.bfloat16
MASKED = -1e30
FLOOR = -1e20
LOG2E = math.log2(math.e)
NT = (((1,), (1,)), ((), ()))


def dot(a, b):
    return jnp.dot(a, b, preferred_element_type=F32)


def dot_nt(a, b):
    return lax.dot_general(a, b, NT, preferred_element_type=F32)


def iota(shape, dim):
    return lax.broadcasted_iota(jnp.int32, shape, dim)


def spread(shape, query_dim, width, first):
    query = iota(shape, query_dim) * width
    lane = iota(shape, 1 - query_dim) + first
    return (query <= lane) & (lane < query + width)


def start_all(axis, n, me, source, slot, send, recv):
    copies = []
    for o in range(1, n):
        dest = lax.rem(me + o, n)
        copy = pltpu.make_async_remote_copy(
            src_ref=source(dest),
            dst_ref=slot(o),
            send_sem=send.at[o],
            recv_sem=recv.at[o],
            device_id={axis: dest},
            device_id_type=MESH,
        )
        copy.start()
        copies.append(copy)
    return copies


def kernel(
    nc, nh, hl, jl, queries,
    q_hbm, latt_ref, iq_ref, ik_ref, w_ref, pos_ref,
    gq_out, gk_out, gw_out,
    q_buf, e_buf, inner_buf, lg_part, lg_recv, lgq,
    lsh, lsh_recv, lsc, lsc_recv, mst, mst_recv, t_acc, t_part, tg_send, tg_recv,
    gr_all, gk_acc, gk_send, gk_recv, gq_f, gq_send, gq_recv, gw_send, gw_recv, ikt, lat_ref,
    q_sem, lg_s, lg_r, lsh_s, lsh_r, lsc_s, lsc_r, mst_s, mst_r, tg_s, tg_r,
    gr_s, gr_r, gk_s, gk_r, gq_s, gq_r, gw_s, gw_r,
):
    rows = latt_ref.shape[1]
    share = rows // nh
    pair = LANES // queries
    blocks = queries * hl // LANES
    jblocks = queries * jl // LANES
    drows = queries * jl // nc
    chunks = blocks // GROUP
    c = lax.axis_index("ctx")
    h = lax.axis_index("head")
    scale2 = LOG2E / math.sqrt(QK_HEAD)
    own = pl.ds(pl.multiple_of(h * share, share), share)
    base = c * rows
    own_base = base + h * share

    load_q = pltpu.make_async_copy(q_hbm, q_buf, q_sem)
    load_q.start()

    barrier = pltpu.get_barrier_semaphore()
    for o in range(1, nc):
        pl.semaphore_signal(barrier, inc=1, device_id={"ctx": lax.rem(c + o, nc)}, device_id_type=MESH)
    for o in range(1, nh):
        pl.semaphore_signal(barrier, inc=1, device_id={"head": lax.rem(h + o, nh)}, device_id_type=MESH)

    lg_part[...] = jnp.zeros_like(lg_part)

    def logit_block(b, carry):
        at = pl.ds(pl.multiple_of(b * LANES, LANES), LANES)
        inner = dot_nt(ik_ref[...], iq_ref[at, :])
        inner_buf[b] = inner
        p = jnp.maximum(inner, 0.0) * w_ref[pl.ds(b, 1), :]
        pick = jnp.where(spread((LANES, queries), 1, jl, b * LANES), 1.0, 0.0).astype(BF16)
        hi = p.astype(BF16)
        rest = p - hi.astype(F32)
        mid = rest.astype(BF16)
        low = (rest - mid.astype(F32)).astype(BF16)
        lg_part[...] += dot(hi, pick) + dot(mid, pick) + dot(low, pick)
        return carry

    lax.fori_loop(0, jblocks, logit_block, 0)
    ikt[...] = ik_ref[...].astype(F32).T.astype(BF16)
    lat_ref[...] = latt_ref[...].T
    limit = jnp.concatenate([pos_ref[...] - base] * pair, axis=1)

    pl.semaphore_wait(barrier, nc - 1 + nh - 1)

    def head_rows(ref):
        return lambda d: ref.at[pl.ds(pl.multiple_of(d * share, share), share), :]

    pending = []
    lg_copies = start_all("head", nh, h, head_rows(lg_part), lambda o: lg_recv.at[o], lg_s, lg_r)
    pending += lg_copies
    load_q.wait()

    def score_chunk(k):
        def score_block(i, carry):
            b = k * GROUP + i
            q = jnp.concatenate([q_buf[b * pair + p] for p in range(pair)], axis=1)
            s = dot(lat_ref[...], q)
            s = jnp.where(iota(s.shape, 0) <= limit, s, MASKED)
            m = jnp.maximum(jnp.max(s, axis=0, keepdims=True), FLOOR)
            e = jnp.exp2((s - m) * scale2)
            e_buf[b] = e.astype(BF16)
            mst[k, pl.ds(i, 1), :] = m
            mst[k, pl.ds(GROUP + i, 1), :] = jnp.sum(e, axis=0, keepdims=True)
            return carry

        lax.fori_loop(0, GROUP, score_block, 0)
        return start_all(
            "ctx", nc, c, lambda d: mst.at[k], lambda o: mst_recv.at[k, o], mst_s.at[k], mst_r.at[k]
        )

    def logit_stats():
        for copy in lg_copies:
            copy.wait_recv()
        total = lg_part[own, :]
        for o in range(1, nh):
            total = total + lg_recv[o]
        total = jnp.where(iota(total.shape, 0) <= pos_ref[...] - own_base, total, MASKED)
        lgq[...] = total
        m = jnp.maximum(jnp.max(total, axis=0, keepdims=True), FLOOR)
        lsh[0:1, :] = m
        lsh[1:2, :] = jnp.sum(jnp.exp2((total - m) * LOG2E), axis=0, keepdims=True)
        return start_all("head", nh, h, lambda d: lsh, lambda o: lsh_recv.at[o], lsh_s, lsh_r)

    def combine(mine, others):
        m = mine[0:1, :]
        for other in others:
            m = jnp.maximum(m, other[0:1, :])
        total = mine[1:2, :] * jnp.exp2((mine[0:1, :] - m) * LOG2E)
        for other in others:
            total = total + other[1:2, :] * jnp.exp2((other[0:1, :] - m) * LOG2E)
        return m, total

    def logit_stats_ctx(copies):
        for copy in copies:
            copy.wait_recv()
        m, total = combine(lsh[...], [lsh_recv[o] for o in range(1, nh)])
        lsc[0:1, :] = m
        lsc[1:2, :] = total
        return start_all("ctx", nc, c, lambda d: lsc, lambda o: lsc_recv.at[o], lsc_s, lsc_r)

    lsh[...] = jnp.zeros_like(lsh)
    lsc[...] = jnp.zeros_like(lsc)
    mst_copies = []
    lsh_copies = lsc_copies = None
    for k in range(chunks):
        mst_copies.append(score_chunk(k))
        if k == min(1, chunks - 1):
            lsh_copies = logit_stats()
        if k == min(2, chunks - 1):
            lsc_copies = logit_stats_ctx(lsh_copies)
    pending += lsh_copies + lsc_copies
    for copies in mst_copies:
        pending += copies

    t_acc[...] = jnp.zeros_like(t_acc)
    same = lax.rem(iota((queries, LANES), 1), queries) == iota((queries, LANES), 0)
    for k in range(chunks):
        for copy in mst_copies[k]:
            copy.wait_recv()
        mine = mst[k]
        highest = mine[:GROUP]
        for o in range(1, nc):
            highest = jnp.maximum(highest, mst_recv[k, o, :GROUP, :])
        shift = jnp.exp2((mine[:GROUP] - highest) * scale2)
        total = mine[GROUP:] * shift
        for o in range(1, nc):
            total = total + mst_recv[k, o, GROUP:, :] * jnp.exp2(
                (mst_recv[k, o, :GROUP, :] - highest) * scale2
            )
        factor = shift / total
        for i in range(GROUP):
            b = k * GROUP + i
            full = jnp.where(same, factor[i : i + 1, :], 0.0)
            hi = full.astype(BF16)
            low = (full - hi.astype(F32)).astype(BF16)
            t_acc[...] += dot_nt(e_buf[b], jnp.concatenate([hi, low], axis=0))
    t_part[...] = t_acc[:, :queries] + t_acc[:, queries:]
    tg_send[...] = t_part[...].astype(BF16)
    tg_copies = start_all("head", nh, h, head_rows(tg_send), lambda o: tg_recv.at[o], tg_s, tg_r)
    pending += tg_copies

    for copy in lsc_copies:
        copy.wait_recv()
    high, total = combine(lsc[...], [lsc_recv[o] for o in range(1, nc)])
    logits = lgq[...]
    predicted = jnp.exp2((logits - high) * LOG2E) * (1.0 / total)
    for copy in tg_copies:
        copy.wait_recv()
    target = t_part[own, :]
    for o in range(1, nh):
        target = target + tg_recv[o].astype(F32)
    gradient = jnp.where(
        iota(target.shape, 0) <= pos_ref[...] - own_base,
        math.sqrt(rows * nc) * (predicted - target * (1.0 / HEADS)),
        0.0,
    )
    gr_all[own, :] = gradient.astype(BF16)
    gr_copies = start_all("head", nh, h, lambda d: gr_all.at[own, :], lambda o: gr_all.at[own, :], gr_s, gr_r)
    pending += gr_copies
    for copy in gr_copies:
        copy.wait_recv()

    gk_acc[...] = jnp.zeros_like(gk_acc)

    def grad_block(b):
        at = pl.ds(pl.multiple_of(b * LANES, LANES), LANES)
        pick = jnp.where(spread((queries, LANES), 0, jl, b * LANES), 1.0, 0.0).astype(BF16)
        grad = dot(gr_all[...], pick)
        inner = inner_buf[b]
        gw_send[pl.ds(b, 1), :] = jnp.sum(grad * jnp.maximum(inner, 0.0), axis=0, keepdims=True)
        delta = jnp.where(inner > 0, grad * w_ref[pl.ds(b, 1), :], 0.0).astype(BF16)
        gk_acc[...] += dot(delta, iq_ref[at, :])
        block = dot(ikt[...], delta).T
        gq_f[at, :] = block
        gq_send[at, :] = block.astype(BF16)

    def gq_copy(o):
        dest = lax.rem(c + o, nc)
        return pltpu.make_async_remote_copy(
            src_ref=gq_send.at[pl.ds(pl.multiple_of(dest * drows, drows), drows), :],
            dst_ref=gq_recv.at[o],
            send_sem=gq_s.at[o],
            recv_sem=gq_r.at[o],
            device_id={"ctx": dest},
            device_id_type=MESH,
        )

    if jblocks == nc:
        def grad_step(o, carry):
            grad_block(lax.rem(c + o, nc))
            gq_copy(o).start()
            return carry

        lax.fori_loop(1, nc, grad_step, 0)
        grad_block(c)
    else:
        def grad_step(b, carry):
            grad_block(b)
            return carry

        lax.fori_loop(0, jblocks, grad_step, 0)
        for o in range(1, nc):
            gq_copy(o).start()
    gk_send[...] = gk_acc[...].astype(BF16)
    gk_copies = start_all("head", nh, h, head_rows(gk_send), lambda o: gk_recv.at[o], gk_s, gk_r)
    gw_copies = start_all("ctx", nc, c, lambda d: gw_send, lambda o: gw_recv.at[o], gw_s, gw_r)
    gq_copies = [gq_copy(o) for o in range(1, nc)]
    pending += gk_copies + gw_copies + gq_copies

    for copy in gk_copies:
        copy.wait_recv()
    total = gk_acc[own, :]
    for o in range(1, nh):
        total = total + gk_recv[o].astype(F32)
    gk_out[...] = total
    for copy in gq_copies:
        copy.wait_recv()
    total = gq_f[pl.ds(pl.multiple_of(c * drows, drows), drows), :]
    for o in range(1, nc):
        total = total + gq_recv[o].astype(F32)
    gq_out[...] = total
    for copy in gw_copies:
        copy.wait_recv()
    total = gw_send[...]
    for o in range(1, nc):
        total = total + gw_recv[o]
    gw_out[...] = total
    for copy in pending:
        copy.wait_send()


def local(nc, nh, positions, mla_queries, latent_keys, index_queries, index_keys, head_weights):
    queries, hl, dqk = mla_queries.shape
    _, jl, di = index_queries.shape
    rows = latent_keys.shape[0]
    share = rows // nh
    blocks = queries * hl // LANES
    jblocks = queries * jl // LANES
    chunks = blocks // GROUP
    own = queries // nc
    drows = own * jl
    q = mla_queries.transpose(1, 2, 0)
    iq = index_queries.reshape(queries * jl, di)
    w = head_weights.reshape(jblocks, LANES)
    vm = pltpu.VMEM
    dma = pltpu.SemaphoreType.DMA
    vspec = pl.BlockSpec(memory_space=pltpu.VMEM)
    gq, gk, gw = pl.pallas_call(
        functools.partial(kernel, nc, nh, hl, jl, queries),
        out_shape=(
            jax.ShapeDtypeStruct((drows, di), F32),
            jax.ShapeDtypeStruct((share, di), F32),
            jax.ShapeDtypeStruct((jblocks, LANES), F32),
        ),
        in_specs=[pl.BlockSpec(memory_space=pl.ANY)] + [vspec] * 5,
        out_specs=(vspec, vspec, vspec),
        scratch_shapes=[
            vm((hl, dqk, queries), BF16),
            vm((blocks, rows, LANES), BF16),
            vm((jblocks, rows, LANES), F32),
            vm((rows, queries), F32),
            vm((nh, share, queries), F32),
            vm((share, queries), F32),
            vm((8, queries), F32),
            vm((nh, 8, queries), F32),
            vm((8, queries), F32),
            vm((nc, 8, queries), F32),
            vm((chunks, 2 * GROUP, LANES), F32),
            vm((chunks, nc, 2 * GROUP, LANES), F32),
            vm((rows, 2 * queries), F32),
            vm((rows, queries), F32),
            vm((rows, queries), BF16),
            vm((nh, share, queries), BF16),
            vm((rows, queries), BF16),
            vm((rows, di), F32),
            vm((rows, di), BF16),
            vm((nh, share, di), BF16),
            vm((queries * jl, di), F32),
            vm((queries * jl, di), BF16),
            vm((nc, drows, di), BF16),
            vm((jblocks, LANES), F32),
            vm((nc, jblocks, LANES), F32),
            vm((di, rows), BF16),
            vm((rows, dqk), BF16),
            dma,
            dma((nh,)), dma((nh,)),
            dma((nh,)), dma((nh,)),
            dma((nc,)), dma((nc,)),
            dma((chunks, nc)), dma((chunks, nc)),
            dma((nh,)), dma((nh,)),
            dma((nh,)), dma((nh,)),
            dma((nh,)), dma((nh,)),
            dma((nc,)), dma((nc,)),
            dma((nc,)), dma((nc,)),
        ],
        compiler_params=pltpu.CompilerParams(
            collective_id=0, has_side_effects=True, vmem_limit_bytes=60 * 1024 * 1024
        ),
    )(q, latent_keys.T, iq, index_keys, w, positions.reshape(1, queries))
    gw = lax.dynamic_slice_in_dim(gw.reshape(queries, jl), lax.axis_index("ctx") * own, own, 0)
    return gq.reshape(own, jl, di), gk, gw


def solution(mesh):
    in_specs = (
        P(),
        P(None, "head", None),
        P("ctx", None),
        P(None, "head", None),
        P("ctx", None),
        P(None, "head"),
    )
    out_specs = (P("ctx", "head", None), P(("ctx", "head"), None), P("ctx", "head"))
    body = functools.partial(local, mesh.shape["ctx"], mesh.shape["head"])
    return jax.shard_map(body, mesh=mesh, in_specs=in_specs, out_specs=out_specs, check_vma=False)
```

```python
import functools
import math

import jax
import jax.numpy as jnp
from jax import lax
from jax.experimental import pallas as pl
from jax.experimental.pallas import tpu as pltpu
from jax.sharding import PartitionSpec as P

HEADS = 128
QK_HEAD = 192
LANES = 256
GROUP = 4
MESH = pl.DeviceIdType.MESH
F32 = jnp.float32
BF16 = jnp.bfloat16
MASKED = -1e30
FLOOR = -1e20
LOG2E = math.log2(math.e)
NT = (((1,), (1,)), ((), ()))


def dot(a, b):
    return jnp.dot(a, b, preferred_element_type=F32)


def dot_nt(a, b):
    return lax.dot_general(a, b, NT, preferred_element_type=F32)


def iota(shape, dim):
    return lax.broadcasted_iota(jnp.int32, shape, dim)


def spread(shape, query_dim, width, first):
    query = iota(shape, query_dim) * width
    lane = iota(shape, 1 - query_dim) + first
    return (query <= lane) & (lane < query + width)


def terms(x):
    hi = x.astype(BF16)
    rest = x - hi.astype(F32)
    mid = rest.astype(BF16)
    return hi, mid, (rest - mid.astype(F32)).astype(BF16)


def start_all(axis, n, me, source, slot, send, recv):
    copies = []
    for o in range(1, n):
        dest = lax.rem(me + o, n)
        copy = pltpu.make_async_remote_copy(
            src_ref=source(dest),
            dst_ref=slot(o),
            send_sem=send.at[o],
            recv_sem=recv.at[o],
            device_id={axis: dest},
            device_id_type=MESH,
        )
        copy.start()
        copies.append(copy)
    return copies


def kernel(
    nc, nh, hl, jl, queries,
    q_hbm, latt_ref, iq_ref, ik_ref, wt_ref, pos_ref,
    gq_out, gk_out, gw_out,
    q_buf, e_buf, inner_buf, lg_part, lg_recv, lgq,
    lsh, lsh_recv, lsc, lsc_recv, mst, mst_recv, t_acc, t_part, tg_send, tg_recv,
    gr_all, gk_acc, gk_send, gk_recv, gq_f, gq_send, gq_recv, gw_send, gw_recv, ikt, lat_ref, w_ref, s_even, s_odd,
    q_sem, lg_s, lg_r, lsh_s, lsh_r, lsc_s, lsc_r, mst_s, mst_r, tg_s, tg_r,
    gr_s, gr_r, gk_s, gk_r, gq_s, gq_r, gw_s, gw_r,
):
    rows = latt_ref.shape[1]
    share = rows // nh
    pair = LANES // queries
    blocks = queries * hl // LANES
    jblocks = queries * jl // LANES
    drows = queries * jl // nc
    chunks = blocks // GROUP
    c = lax.axis_index("ctx")
    h = lax.axis_index("head")
    scale2 = LOG2E / math.sqrt(QK_HEAD)
    own = pl.ds(pl.multiple_of(h * share, share), share)
    base = c * rows
    own_base = base + h * share

    load_q = pltpu.make_async_copy(q_hbm, q_buf, q_sem)
    load_q.start()

    barrier = pltpu.get_barrier_semaphore()
    for o in range(1, nc):
        pl.semaphore_signal(barrier, inc=1, device_id={"ctx": lax.rem(c + o, nc)}, device_id_type=MESH)
    for o in range(1, nh):
        pl.semaphore_signal(barrier, inc=1, device_id={"head": lax.rem(h + o, nh)}, device_id_type=MESH)

    lg_part[...] = jnp.zeros_like(lg_part)

    def logit_block(b, carry):
        at = pl.ds(pl.multiple_of(b * LANES, LANES), LANES)
        inner = dot_nt(ik_ref[...], iq_ref[at, :])
        inner_buf[b] = inner
        across = jnp.where(spread((queries, LANES), 0, jl, b * LANES), 1.0, 0.0).astype(BF16)
        weights = sum(dot(term, across) for term in terms(wt_ref[...]))
        head = lax.rem(iota((jl, LANES), 1), jl)
        weights = jnp.where(head == iota((jl, LANES), 0), weights, 0.0)
        weights = jnp.sum(weights, axis=0, keepdims=True)
        w_ref[pl.ds(b, 1), :] = weights
        p = jnp.maximum(inner, 0.0) * weights
        pick = jnp.where(spread((LANES, queries), 1, jl, b * LANES), 1.0, 0.0).astype(BF16)
        lg_part[...] += dot(jnp.concatenate(terms(p), axis=1), jnp.concatenate([pick] * 3, axis=0))
        return carry

    lax.fori_loop(0, jblocks, logit_block, 0)
    ikt[...] = ik_ref[...].astype(F32).T.astype(BF16)
    lat_ref[...] = latt_ref[...].T
    limit = jnp.concatenate([pos_ref[...] - base] * pair, axis=1)

    pl.semaphore_wait(barrier, nc - 1 + nh - 1)

    def head_rows(ref):
        return lambda d: ref.at[pl.ds(pl.multiple_of(d * share, share), share), :]

    pending = []
    lg_copies = start_all("head", nh, h, head_rows(lg_part), lambda o: lg_recv.at[o], lg_s, lg_r)
    pending += lg_copies
    load_q.wait()

    def scores(b, out):
        q = jnp.concatenate([q_buf[b * pair + p] for p in range(pair)], axis=1)
        s = dot(lat_ref[...], q)
        s = jnp.where(iota(s.shape, 0) <= limit, s, MASKED)
        out[...] = s
        return jnp.maximum(jnp.max(s, axis=0, keepdims=True), FLOOR)

    def exponentials(k, i, src, m):
        e = jnp.exp2((src[...] - m) * scale2)
        e_buf[k * GROUP + i] = e.astype(BF16)
        mst[k, pl.ds(i, 1), :] = m
        mst[k, pl.ds(GROUP + i, 1), :] = jnp.sum(e, axis=0, keepdims=True)

    def score_chunk(k, m):
        def score_pair(j, m):
            b = k * GROUP + 2 * j
            m_odd = scores(b + 1, s_odd)
            exponentials(k, 2 * j, s_even, m)
            m_even = scores(lax.rem(b + 2, blocks), s_even)
            exponentials(k, 2 * j + 1, s_odd, m_odd)
            return m_even

        m = lax.fori_loop(0, GROUP // 2, score_pair, m)
        return m, score_send(k)

    def score_send(k):
        return start_all(
            "ctx", nc, c, lambda d: mst.at[k], lambda o: mst_recv.at[k, o], mst_s.at[k], mst_r.at[k]
        )

    def logit_stats():
        for copy in lg_copies:
            copy.wait_recv()
        total = lg_part[own, :]
        for o in range(1, nh):
            total = total + lg_recv[o]
        total = jnp.where(iota(total.shape, 0) <= pos_ref[...] - own_base, total, MASKED)
        lgq[...] = total
        m = jnp.maximum(jnp.max(total, axis=0, keepdims=True), FLOOR)
        lsh[0:1, :] = m
        lsh[1:2, :] = jnp.sum(jnp.exp2((total - m) * LOG2E), axis=0, keepdims=True)
        return start_all("head", nh, h, lambda d: lsh, lambda o: lsh_recv.at[o], lsh_s, lsh_r)

    def combine(mine, others):
        m = mine[0:1, :]
        for other in others:
            m = jnp.maximum(m, other[0:1, :])
        total = mine[1:2, :] * jnp.exp2((mine[0:1, :] - m) * LOG2E)
        for other in others:
            total = total + other[1:2, :] * jnp.exp2((other[0:1, :] - m) * LOG2E)
        return m, total

    def logit_stats_ctx(copies):
        for copy in copies:
            copy.wait_recv()
        m, total = combine(lsh[...], [lsh_recv[o] for o in range(1, nh)])
        lsc[0:1, :] = m
        lsc[1:2, :] = total
        return start_all("ctx", nc, c, lambda d: lsc, lambda o: lsc_recv.at[o], lsc_s, lsc_r)

    lsh[...] = jnp.zeros_like(lsh)
    lsc[...] = jnp.zeros_like(lsc)
    mst_copies = []
    high = scores(0, s_even)
    lsh_copies = lsc_copies = None
    for k in range(chunks):
        high, copies = score_chunk(k, high)
        mst_copies.append(copies)
        if k == min(1, chunks - 1):
            lsh_copies = logit_stats()
        if k == min(2, chunks - 1):
            lsc_copies = logit_stats_ctx(lsh_copies)
    pending += lsh_copies + lsc_copies
    for copies in mst_copies:
        pending += copies

    t_acc[...] = jnp.zeros_like(t_acc)
    same = lax.rem(iota((queries, LANES), 1), queries) == iota((queries, LANES), 0)
    for k in range(chunks):
        for copy in mst_copies[k]:
            copy.wait_recv()
        mine = mst[k]
        highest = mine[:GROUP]
        for o in range(1, nc):
            highest = jnp.maximum(highest, mst_recv[k, o, :GROUP, :])
        shift = jnp.exp2((mine[:GROUP] - highest) * scale2)
        total = mine[GROUP:] * shift
        for o in range(1, nc):
            total = total + mst_recv[k, o, GROUP:, :] * jnp.exp2(
                (mst_recv[k, o, :GROUP, :] - highest) * scale2
            )
        factor = shift / total
        for i in range(GROUP):
            b = k * GROUP + i
            full = jnp.where(same, factor[i : i + 1, :], 0.0)
            hi = full.astype(BF16)
            low = (full - hi.astype(F32)).astype(BF16)
            t_acc[...] += dot_nt(e_buf[b], jnp.concatenate([hi, low], axis=0))
    t_part[...] = t_acc[:, :queries] + t_acc[:, queries:]
    tg_send[...] = t_part[...].astype(BF16)
    tg_copies = start_all("head", nh, h, head_rows(tg_send), lambda o: tg_recv.at[o], tg_s, tg_r)
    pending += tg_copies

    for copy in lsc_copies:
        copy.wait_recv()
    high, total = combine(lsc[...], [lsc_recv[o] for o in range(1, nc)])
    logits = lgq[...]
    predicted = jnp.exp2((logits - high) * LOG2E) * (1.0 / total)
    for copy in tg_copies:
        copy.wait_recv()
    target = t_part[own, :]
    for o in range(1, nh):
        target = target + tg_recv[o].astype(F32)
    gradient = jnp.where(
        iota(target.shape, 0) <= pos_ref[...] - own_base,
        math.sqrt(rows * nc) * (predicted - target * (1.0 / HEADS)),
        0.0,
    )
    gr_all[own, :] = gradient.astype(BF16)
    gr_copies = start_all("head", nh, h, lambda d: gr_all.at[own, :], lambda o: gr_all.at[own, :], gr_s, gr_r)
    pending += gr_copies
    for copy in gr_copies:
        copy.wait_recv()

    gk_acc[...] = jnp.zeros_like(gk_acc)

    def grad_block(b):
        at = pl.ds(pl.multiple_of(b * LANES, LANES), LANES)
        pick = jnp.where(spread((queries, LANES), 0, jl, b * LANES), 1.0, 0.0).astype(BF16)
        grad = dot(gr_all[...], pick)
        inner = inner_buf[b]
        gw_send[pl.ds(b, 1), :] = jnp.sum(grad * jnp.maximum(inner, 0.0), axis=0, keepdims=True)
        delta = jnp.where(inner > 0, grad * w_ref[pl.ds(b, 1), :], 0.0).astype(BF16)
        gk_acc[...] += dot(delta, iq_ref[at, :])
        block = dot(ikt[...], delta).T
        gq_f[at, :] = block
        gq_send[at, :] = block.astype(BF16)

    def gq_copy(o):
        dest = lax.rem(c + o, nc)
        return pltpu.make_async_remote_copy(
            src_ref=gq_send.at[pl.ds(pl.multiple_of(dest * drows, drows), drows), :],
            dst_ref=gq_recv.at[o],
            send_sem=gq_s.at[o],
            recv_sem=gq_r.at[o],
            device_id={"ctx": dest},
            device_id_type=MESH,
        )

    if jblocks == nc:
        def grad_step(o, carry):
            grad_block(lax.rem(c + o, nc))
            gq_copy(o).start()
            return carry

        lax.fori_loop(1, nc, grad_step, 0)
        grad_block(c)
    else:
        def grad_step(b, carry):
            grad_block(b)
            return carry

        lax.fori_loop(0, jblocks, grad_step, 0)
        for o in range(1, nc):
            gq_copy(o).start()
    gk_send[...] = gk_acc[...].astype(BF16)
    gk_copies = start_all("head", nh, h, head_rows(gk_send), lambda o: gk_recv.at[o], gk_s, gk_r)
    gw_copies = start_all("ctx", nc, c, lambda d: gw_send, lambda o: gw_recv.at[o], gw_s, gw_r)
    gq_copies = [gq_copy(o) for o in range(1, nc)]
    pending += gk_copies + gw_copies + gq_copies

    for copy in gk_copies:
        copy.wait_recv()
    total = gk_acc[own, :]
    for o in range(1, nh):
        total = total + gk_recv[o].astype(F32)
    gk_out[...] = total
    for copy in gq_copies:
        copy.wait_recv()
    total = gq_f[pl.ds(pl.multiple_of(c * drows, drows), drows), :]
    for o in range(1, nc):
        total = total + gq_recv[o].astype(F32)
    gq_out[...] = total
    for copy in gw_copies:
        copy.wait_recv()
    total = gw_send[...]
    for o in range(1, nc):
        total = total + gw_recv[o]
    picked = jnp.zeros((queries // nc, LANES), F32)
    for b in range(jblocks):
        mine = spread(picked.shape, 0, jl, b * LANES - c * drows)
        picked = picked + jnp.where(mine, total[b : b + 1, :], 0.0)
    head = lax.rem(iota((LANES, jl), 0), jl) == iota((LANES, jl), 1)
    head = jnp.where(head, 1.0, 0.0).astype(BF16)
    gw_out[...] = sum(dot(term, head) for term in terms(picked))
    for copy in pending:
        copy.wait_send()


def finish(a_ref, b_ref, c_ref, a_out, b_out, c_out):
    a_out[...] = a_ref[...]
    b_out[...] = b_ref[...]
    c_out[...] = c_ref[...]


def local(nc, nh, positions, mla_queries, latent_keys, index_queries, index_keys, head_weights):
    queries, hl, dqk = mla_queries.shape
    _, jl, di = index_queries.shape
    rows = latent_keys.shape[0]
    share = rows // nh
    blocks = queries * hl // LANES
    jblocks = queries * jl // LANES
    chunks = blocks // GROUP
    own = queries // nc
    drows = own * jl
    q = mla_queries.transpose(1, 2, 0)
    iq = index_queries.reshape(queries * jl, di)
    vm = pltpu.VMEM
    dma = pltpu.SemaphoreType.DMA
    vspec = pl.BlockSpec(memory_space=pltpu.VMEM)
    gq, gk, gw = pl.pallas_call(
        functools.partial(kernel, nc, nh, hl, jl, queries),
        out_shape=(
            jax.ShapeDtypeStruct((drows, di), F32),
            jax.ShapeDtypeStruct((share, di), F32),
            jax.ShapeDtypeStruct((own, jl), F32),
        ),
        in_specs=[pl.BlockSpec(memory_space=pl.ANY)] + [vspec] * 5,
        out_specs=(vspec, vspec, vspec),
        scratch_shapes=[
            vm((hl, dqk, queries), BF16),
            vm((blocks, rows, LANES), BF16),
            vm((jblocks, rows, LANES), F32),
            vm((rows, queries), F32),
            vm((nh, share, queries), F32),
            vm((share, queries), F32),
            vm((8, queries), F32),
            vm((nh, 8, queries), F32),
            vm((8, queries), F32),
            vm((nc, 8, queries), F32),
            vm((chunks, 2 * GROUP, LANES), F32),
            vm((chunks, nc, 2 * GROUP, LANES), F32),
            vm((rows, 2 * queries), F32),
            vm((rows, queries), F32),
            vm((rows, queries), BF16),
            vm((nh, share, queries), BF16),
            vm((rows, queries), BF16),
            vm((rows, di), F32),
            vm((rows, di), BF16),
            vm((nh, share, di), BF16),
            vm((queries * jl, di), F32),
            vm((queries * jl, di), BF16),
            vm((nc, drows, di), BF16),
            vm((jblocks, LANES), F32),
            vm((nc, jblocks, LANES), F32),
            vm((di, rows), BF16),
            vm((rows, dqk), BF16),
            vm((jblocks, LANES), F32),
            vm((rows, LANES), F32),
            vm((rows, LANES), F32),
            dma,
            dma((nh,)), dma((nh,)),
            dma((nh,)), dma((nh,)),
            dma((nc,)), dma((nc,)),
            dma((chunks, nc)), dma((chunks, nc)),
            dma((nh,)), dma((nh,)),
            dma((nh,)), dma((nh,)),
            dma((nh,)), dma((nh,)),
            dma((nc,)), dma((nc,)),
            dma((nc,)), dma((nc,)),
        ],
        compiler_params=pltpu.CompilerParams(
            collective_id=0, has_side_effects=True, vmem_limit_bytes=60 * 1024 * 1024
        ),
    )(q, latent_keys.T, iq, index_keys, head_weights.T, positions.reshape(1, queries))
    gq, gk, gw = pl.pallas_call(
        finish,
        out_shape=tuple(jax.ShapeDtypeStruct(x.shape, F32) for x in (gq, gk, gw)),
        in_specs=[vspec] * 3,
        out_specs=(vspec,) * 3,
    )(gq, gk, gw)
    return gq.reshape(own, jl, di), gk, gw


def solution(mesh):
    in_specs = (
        P(),
        P(None, "head", None),
        P("ctx", None),
        P(None, "head", None),
        P("ctx", None),
        P(None, "head"),
    )
    out_specs = (P("ctx", "head", None), P(("ctx", "head"), None), P("ctx", "head"))
    body = functools.partial(local, mesh.shape["ctx"], mesh.shape["head"])
    return jax.shard_map(body, mesh=mesh, in_specs=in_specs, out_specs=out_specs, check_vma=False)
```

```python
import functools
import math

import jax
import jax.numpy as jnp
from jax import lax
from jax.experimental import pallas as pl
from jax.experimental.pallas import tpu as pltpu
from jax.sharding import PartitionSpec as P

HEADS = 128
QK_HEAD = 192
LANES = 256
GROUP = 4
MESH = pl.DeviceIdType.MESH
F32 = jnp.float32
BF16 = jnp.bfloat16
MASKED = -1e30
FLOOR = -1e20
LOG2E = math.log2(math.e)
NT = (((1,), (1,)), ((), ()))


def dot(a, b):
    return jnp.dot(a, b, preferred_element_type=F32)


def dot_nt(a, b):
    return lax.dot_general(a, b, NT, preferred_element_type=F32)


def iota(shape, dim):
    return lax.broadcasted_iota(jnp.int32, shape, dim)


def spread(shape, query_dim, width, first):
    query = iota(shape, query_dim) * width
    lane = iota(shape, 1 - query_dim) + first
    return (query <= lane) & (lane < query + width)


def terms(x):
    hi = x.astype(BF16)
    rest = x - hi.astype(F32)
    mid = rest.astype(BF16)
    return hi, mid, (rest - mid.astype(F32)).astype(BF16)


def start_all(axis, n, me, source, slot, send, recv):
    copies = []
    for o in range(1, n):
        dest = lax.rem(me + o, n)
        copy = pltpu.make_async_remote_copy(
            src_ref=source(dest),
            dst_ref=slot(o),
            send_sem=send.at[o],
            recv_sem=recv.at[o],
            device_id={axis: dest},
            device_id_type=MESH,
        )
        copy.start()
        copies.append(copy)
    return copies


def kernel(
    nc, nh, hl, jl, queries,
    q_hbm, latt_ref, iq_ref, ik_ref, wt_ref, pos_ref,
    gq_out, gk_out, gw_out,
    q_buf, e_buf, inner_buf, lg_part, lg_recv, lgq,
    lsh, lsh_recv, lsc, lsc_recv, mst, mst_recv, t_acc, t_part, tg_send, tg_recv,
    gr_all, gk_acc, gk_send, gk_recv, gq_f, gq_send, gq_recv, gw_send, gw_recv, ikt, lat_ref, w_ref, s_even, s_odd,
    q_sem, lg_s, lg_r, lsh_s, lsh_r, lsc_s, lsc_r, mst_s, mst_r, tg_s, tg_r,
    gr_s, gr_r, gk_s, gk_r, gq_s, gq_r, gw_s, gw_r,
):
    rows = latt_ref.shape[1]
    share = rows // nh
    pair = LANES // queries
    blocks = queries * hl // LANES
    jblocks = queries * jl // LANES
    drows = queries * jl // nc
    chunks = blocks // GROUP
    c = lax.axis_index("ctx")
    h = lax.axis_index("head")
    scale2 = LOG2E / math.sqrt(QK_HEAD)
    own = pl.ds(pl.multiple_of(h * share, share), share)
    base = c * rows
    own_base = base + h * share

    load_q = pltpu.make_async_copy(q_hbm, q_buf, q_sem)
    load_q.start()

    barrier = pltpu.get_barrier_semaphore()
    for o in range(1, nc):
        pl.semaphore_signal(barrier, inc=1, device_id={"ctx": lax.rem(c + o, nc)}, device_id_type=MESH)
    for o in range(1, nh):
        pl.semaphore_signal(barrier, inc=1, device_id={"head": lax.rem(h + o, nh)}, device_id_type=MESH)

    lg_part[...] = jnp.zeros_like(lg_part)

    def logit_block(b, carry):
        at = pl.ds(pl.multiple_of(b * LANES, LANES), LANES)
        inner = dot_nt(ik_ref[...], iq_ref[at, :])
        inner_buf[b] = inner
        across = jnp.where(spread((queries, LANES), 0, jl, b * LANES), 1.0, 0.0).astype(BF16)
        weights = sum(dot(term, across) for term in terms(wt_ref[...]))
        head = lax.rem(iota((jl, LANES), 1), jl)
        weights = jnp.where(head == iota((jl, LANES), 0), weights, 0.0)
        weights = jnp.sum(weights, axis=0, keepdims=True)
        w_ref[pl.ds(b, 1), :] = weights
        p = jnp.maximum(inner, 0.0) * weights
        pick = jnp.where(spread((LANES, queries), 1, jl, b * LANES), 1.0, 0.0).astype(BF16)
        lg_part[...] += dot(jnp.concatenate(terms(p), axis=1), jnp.concatenate([pick] * 3, axis=0))
        return carry

    lax.fori_loop(0, jblocks, logit_block, 0)
    ikt[...] = ik_ref[...].astype(F32).T.astype(BF16)
    lat_ref[...] = latt_ref[...].T
    limit = jnp.concatenate([pos_ref[...] - base] * pair, axis=1)

    pl.semaphore_wait(barrier, nc - 1 + nh - 1)

    def head_rows(ref):
        return lambda d: ref.at[pl.ds(pl.multiple_of(d * share, share), share), :]

    pending = []
    lg_copies = start_all("head", nh, h, head_rows(lg_part), lambda o: lg_recv.at[o], lg_s, lg_r)
    pending += lg_copies
    load_q.wait()

    def scores(b, out):
        q = jnp.concatenate([q_buf[b * pair + p] for p in range(pair)], axis=1)
        s = dot(lat_ref[...], q)
        s = jnp.where(iota(s.shape, 0) <= limit, s, MASKED)
        out[...] = s
        return jnp.maximum(jnp.max(s, axis=0, keepdims=True), FLOOR)

    def exponentials(k, i, src, m):
        e = jnp.exp2((src[...] - m) * scale2)
        e_buf[k * GROUP + i] = e.astype(BF16)
        mst[k, pl.ds(i, 1), :] = m
        mst[k, pl.ds(GROUP + i, 1), :] = jnp.sum(e, axis=0, keepdims=True)

    def score_chunk(k, m):
        def score_pair(j, m):
            b = k * GROUP + 2 * j
            m_odd = scores(b + 1, s_odd)
            exponentials(k, 2 * j, s_even, m)
            m_even = scores(lax.rem(b + 2, blocks), s_even)
            exponentials(k, 2 * j + 1, s_odd, m_odd)
            return m_even

        m = lax.fori_loop(0, GROUP // 2, score_pair, m)
        return m, score_send(k)

    def score_send(k):
        return start_all(
            "ctx", nc, c, lambda d: mst.at[k], lambda o: mst_recv.at[k, o], mst_s.at[k], mst_r.at[k]
        )

    def logit_stats():
        for copy in lg_copies:
            copy.wait_recv()
        total = lg_part[own, :]
        for o in range(1, nh):
            total = total + lg_recv[o]
        total = jnp.where(iota(total.shape, 0) <= pos_ref[...] - own_base, total, MASKED)
        lgq[...] = total
        m = jnp.maximum(jnp.max(total, axis=0, keepdims=True), FLOOR)
        lsh[0:1, :] = m
        lsh[1:2, :] = jnp.sum(jnp.exp2((total - m) * LOG2E), axis=0, keepdims=True)
        return start_all("head", nh, h, lambda d: lsh, lambda o: lsh_recv.at[o], lsh_s, lsh_r)

    def combine(mine, others):
        m = mine[0:1, :]
        for other in others:
            m = jnp.maximum(m, other[0:1, :])
        total = mine[1:2, :] * jnp.exp2((mine[0:1, :] - m) * LOG2E)
        for other in others:
            total = total + other[1:2, :] * jnp.exp2((other[0:1, :] - m) * LOG2E)
        return m, total

    def logit_stats_ctx(copies):
        for copy in copies:
            copy.wait_recv()
        m, total = combine(lsh[...], [lsh_recv[o] for o in range(1, nh)])
        lsc[0:1, :] = m
        lsc[1:2, :] = total
        return start_all("ctx", nc, c, lambda d: lsc, lambda o: lsc_recv.at[o], lsc_s, lsc_r)

    lsh[...] = jnp.zeros_like(lsh)
    lsc[...] = jnp.zeros_like(lsc)
    mst_copies = []
    high = scores(0, s_even)
    for k in range(chunks):
        high, copies = score_chunk(k, high)
        mst_copies.append(copies)
    lsh_copies = logit_stats()
    pending += lsh_copies
    for copies in mst_copies:
        pending += copies

    t_acc[...] = jnp.zeros_like(t_acc)
    same = lax.rem(iota((queries, LANES), 1), queries) == iota((queries, LANES), 0)
    for k in range(chunks):
        for copy in mst_copies[k]:
            copy.wait_recv()
        mine = mst[k]
        highest = mine[:GROUP]
        for o in range(1, nc):
            highest = jnp.maximum(highest, mst_recv[k, o, :GROUP, :])
        shift = jnp.exp2((mine[:GROUP] - highest) * scale2)
        total = mine[GROUP:] * shift
        for o in range(1, nc):
            total = total + mst_recv[k, o, GROUP:, :] * jnp.exp2(
                (mst_recv[k, o, :GROUP, :] - highest) * scale2
            )
        factor = shift / total
        for i in range(GROUP):
            b = k * GROUP + i
            full = jnp.where(same, factor[i : i + 1, :], 0.0)
            hi = full.astype(BF16)
            low = (full - hi.astype(F32)).astype(BF16)
            t_acc[...] += dot_nt(e_buf[b], jnp.concatenate([hi, low], axis=0))
        if k == (chunks - 1) // 2:
            lsc_copies = logit_stats_ctx(lsh_copies)
            pending += lsc_copies
    t_part[...] = t_acc[:, :queries] + t_acc[:, queries:]
    tg_send[...] = t_part[...].astype(BF16)
    tg_copies = start_all("head", nh, h, head_rows(tg_send), lambda o: tg_recv.at[o], tg_s, tg_r)
    pending += tg_copies

    for copy in lsc_copies:
        copy.wait_recv()
    high, total = combine(lsc[...], [lsc_recv[o] for o in range(1, nc)])
    logits = lgq[...]
    predicted = jnp.exp2((logits - high) * LOG2E) * (1.0 / total)
    for copy in tg_copies:
        copy.wait_recv()
    target = t_part[own, :]
    for o in range(1, nh):
        target = target + tg_recv[o].astype(F32)
    gradient = jnp.where(
        iota(target.shape, 0) <= pos_ref[...] - own_base,
        math.sqrt(rows * nc) * (predicted - target * (1.0 / HEADS)),
        0.0,
    )
    gr_all[own, :] = gradient.astype(BF16)
    gr_copies = start_all("head", nh, h, lambda d: gr_all.at[own, :], lambda o: gr_all.at[own, :], gr_s, gr_r)
    pending += gr_copies
    for copy in gr_copies:
        copy.wait_recv()

    gk_acc[...] = jnp.zeros_like(gk_acc)

    def grad_block(b):
        at = pl.ds(pl.multiple_of(b * LANES, LANES), LANES)
        pick = jnp.where(spread((queries, LANES), 0, jl, b * LANES), 1.0, 0.0).astype(BF16)
        grad = dot(gr_all[...], pick)
        inner = inner_buf[b]
        gw_send[pl.ds(b, 1), :] = jnp.sum(grad * jnp.maximum(inner, 0.0), axis=0, keepdims=True)
        delta = jnp.where(inner > 0, grad * w_ref[pl.ds(b, 1), :], 0.0).astype(BF16)
        gk_acc[...] += dot(delta, iq_ref[at, :])
        block = dot(ikt[...], delta).T
        gq_f[at, :] = block
        gq_send[at, :] = block.astype(BF16)

    def gq_copy(o):
        dest = lax.rem(c + o, nc)
        return pltpu.make_async_remote_copy(
            src_ref=gq_send.at[pl.ds(pl.multiple_of(dest * drows, drows), drows), :],
            dst_ref=gq_recv.at[o],
            send_sem=gq_s.at[o],
            recv_sem=gq_r.at[o],
            device_id={"ctx": dest},
            device_id_type=MESH,
        )

    if jblocks == nc:
        def grad_step(o, carry):
            grad_block(lax.rem(c + o, nc))
            gq_copy(o).start()
            return carry

        lax.fori_loop(1, nc, grad_step, 0)
        grad_block(c)
    else:
        def grad_step(b, carry):
            grad_block(b)
            return carry

        lax.fori_loop(0, jblocks, grad_step, 0)
        for o in range(1, nc):
            gq_copy(o).start()
    gk_send[...] = gk_acc[...].astype(BF16)
    gk_copies = start_all("head", nh, h, head_rows(gk_send), lambda o: gk_recv.at[o], gk_s, gk_r)
    gw_copies = start_all("ctx", nc, c, lambda d: gw_send, lambda o: gw_recv.at[o], gw_s, gw_r)
    gq_copies = [gq_copy(o) for o in range(1, nc)]
    pending += gk_copies + gw_copies + gq_copies

    for copy in gk_copies:
        copy.wait_recv()
    total = gk_acc[own, :]
    for o in range(1, nh):
        total = total + gk_recv[o].astype(F32)
    gk_out[...] = total
    for copy in gq_copies:
        copy.wait_recv()
    total = gq_f[pl.ds(pl.multiple_of(c * drows, drows), drows), :]
    for o in range(1, nc):
        total = total + gq_recv[o].astype(F32)
    gq_out[...] = total
    for copy in gw_copies:
        copy.wait_recv()
    total = gw_send[...]
    for o in range(1, nc):
        total = total + gw_recv[o]
    picked = jnp.zeros((queries // nc, LANES), F32)
    for b in range(jblocks):
        mine = spread(picked.shape, 0, jl, b * LANES - c * drows)
        picked = picked + jnp.where(mine, total[b : b + 1, :], 0.0)
    head = lax.rem(iota((LANES, jl), 0), jl) == iota((LANES, jl), 1)
    head = jnp.where(head, 1.0, 0.0).astype(BF16)
    gw_out[...] = sum(dot(term, head) for term in terms(picked))
    for copy in pending:
        copy.wait_send()


def finish(a_ref, b_ref, c_ref, a_out, b_out, c_out):
    a_out[...] = a_ref[...]
    b_out[...] = b_ref[...]
    c_out[...] = c_ref[...]


def local(nc, nh, positions, mla_queries, latent_keys, index_queries, index_keys, head_weights):
    queries, hl, dqk = mla_queries.shape
    _, jl, di = index_queries.shape
    rows = latent_keys.shape[0]
    share = rows // nh
    blocks = queries * hl // LANES
    jblocks = queries * jl // LANES
    chunks = blocks // GROUP
    own = queries // nc
    drows = own * jl
    q = mla_queries.transpose(1, 2, 0)
    iq = index_queries.reshape(queries * jl, di)
    vm = pltpu.VMEM
    dma = pltpu.SemaphoreType.DMA
    vspec = pl.BlockSpec(memory_space=pltpu.VMEM)
    gq, gk, gw = pl.pallas_call(
        functools.partial(kernel, nc, nh, hl, jl, queries),
        out_shape=(
            jax.ShapeDtypeStruct((drows, di), F32),
            jax.ShapeDtypeStruct((share, di), F32),
            jax.ShapeDtypeStruct((own, jl), F32),
        ),
        in_specs=[pl.BlockSpec(memory_space=pl.ANY)] + [vspec] * 5,
        out_specs=(vspec, vspec, vspec),
        scratch_shapes=[
            vm((hl, dqk, queries), BF16),
            vm((blocks, rows, LANES), BF16),
            vm((jblocks, rows, LANES), F32),
            vm((rows, queries), F32),
            vm((nh, share, queries), F32),
            vm((share, queries), F32),
            vm((8, queries), F32),
            vm((nh, 8, queries), F32),
            vm((8, queries), F32),
            vm((nc, 8, queries), F32),
            vm((chunks, 2 * GROUP, LANES), F32),
            vm((chunks, nc, 2 * GROUP, LANES), F32),
            vm((rows, 2 * queries), F32),
            vm((rows, queries), F32),
            vm((rows, queries), BF16),
            vm((nh, share, queries), BF16),
            vm((rows, queries), BF16),
            vm((rows, di), F32),
            vm((rows, di), BF16),
            vm((nh, share, di), BF16),
            vm((queries * jl, di), F32),
            vm((queries * jl, di), BF16),
            vm((nc, drows, di), BF16),
            vm((jblocks, LANES), F32),
            vm((nc, jblocks, LANES), F32),
            vm((di, rows), BF16),
            vm((rows, dqk), BF16),
            vm((jblocks, LANES), F32),
            vm((rows, LANES), F32),
            vm((rows, LANES), F32),
            dma,
            dma((nh,)), dma((nh,)),
            dma((nh,)), dma((nh,)),
            dma((nc,)), dma((nc,)),
            dma((chunks, nc)), dma((chunks, nc)),
            dma((nh,)), dma((nh,)),
            dma((nh,)), dma((nh,)),
            dma((nh,)), dma((nh,)),
            dma((nc,)), dma((nc,)),
            dma((nc,)), dma((nc,)),
        ],
        compiler_params=pltpu.CompilerParams(
            collective_id=0, has_side_effects=True, vmem_limit_bytes=60 * 1024 * 1024
        ),
    )(q, latent_keys.T, iq, index_keys, head_weights.T, positions.reshape(1, queries))
    gq, gk, gw = pl.pallas_call(
        finish,
        out_shape=tuple(jax.ShapeDtypeStruct(x.shape, F32) for x in (gq, gk, gw)),
        in_specs=[vspec] * 3,
        out_specs=(vspec,) * 3,
    )(gq, gk, gw)
    return gq.reshape(own, jl, di), gk, gw


def solution(mesh):
    in_specs = (
        P(),
        P(None, "head", None),
        P("ctx", None),
        P(None, "head", None),
        P("ctx", None),
        P(None, "head"),
    )
    out_specs = (P("ctx", "head", None), P(("ctx", "head"), None), P("ctx", "head"))
    body = functools.partial(local, mesh.shape["ctx"], mesh.shape["head"])
    return jax.shard_map(body, mesh=mesh, in_specs=in_specs, out_specs=out_specs, check_vma=False)
```

```python
import functools
import math

import jax
import jax.numpy as jnp
from jax import lax
from jax.experimental import pallas as pl
from jax.experimental.pallas import tpu as pltpu
from jax.sharding import PartitionSpec as P

HEADS = 128
QK_HEAD = 192
LANES = 256
GROUP = 4
MESH = pl.DeviceIdType.MESH
F32 = jnp.float32
BF16 = jnp.bfloat16
MASKED = -1e30
FLOOR = -1e20
LOG2E = math.log2(math.e)
NT = (((1,), (1,)), ((), ()))


def dot(a, b):
    return jnp.dot(a, b, preferred_element_type=F32)


def dot_nt(a, b):
    return lax.dot_general(a, b, NT, preferred_element_type=F32)


def iota(shape, dim):
    return lax.broadcasted_iota(jnp.int32, shape, dim)


def spread(shape, query_dim, width, first):
    query = iota(shape, query_dim) * width
    lane = iota(shape, 1 - query_dim) + first
    return (query <= lane) & (lane < query + width)


def terms(x):
    hi = x.astype(BF16)
    rest = x - hi.astype(F32)
    mid = rest.astype(BF16)
    return hi, mid, (rest - mid.astype(F32)).astype(BF16)


def start_all(axis, n, me, source, slot, send, recv):
    copies = []
    for o in range(1, n):
        dest = lax.rem(me + o, n)
        copy = pltpu.make_async_remote_copy(
            src_ref=source(dest),
            dst_ref=slot(o),
            send_sem=send.at[o],
            recv_sem=recv.at[o],
            device_id={axis: dest},
            device_id_type=MESH,
        )
        copy.start()
        copies.append(copy)
    return copies


def kernel(
    nc, nh, hl, jl, queries,
    q_hbm, latt_ref, iq_ref, ik_ref, wt_ref, pos_ref,
    gq_out, gk_out, gw_out,
    q_buf, e_buf, inner_buf, lg_part, lg_recv, lgq,
    lsh, lsh_recv, lsc, lsc_recv, mst, mst_recv, t_acc, t_part, tg_send, tg_recv,
    gr_all, gk_acc, gk_send, gk_recv, gq_f, gq_send, gq_recv, gw_send, gw_recv, ikt, lat_ref, w_ref, s_even, s_odd, pair_recv, gq_sum,
    q_sem, lg_s, lg_r, lsh_s, lsh_r, lsc_s, lsc_r, mst_s, mst_r, tg_s, tg_r,
    gr_s, gr_r, gk_s, gk_r, gq_s, gq_r, gw_s, gw_r, pair_s, pair_r,
):
    rows = latt_ref.shape[1]
    share = rows // nh
    pair = LANES // queries
    blocks = queries * hl // LANES
    jblocks = queries * jl // LANES
    drows = queries * jl // nc
    chunks = blocks // GROUP
    c = lax.axis_index("ctx")
    h = lax.axis_index("head")
    scale2 = LOG2E / math.sqrt(QK_HEAD)
    own = pl.ds(pl.multiple_of(h * share, share), share)
    base = c * rows
    own_base = base + h * share

    load_q = pltpu.make_async_copy(q_hbm, q_buf, q_sem)
    load_q.start()

    barrier = pltpu.get_barrier_semaphore()
    for o in range(1, nc):
        pl.semaphore_signal(barrier, inc=1, device_id={"ctx": lax.rem(c + o, nc)}, device_id_type=MESH)
    for o in range(1, nh):
        pl.semaphore_signal(barrier, inc=1, device_id={"head": lax.rem(h + o, nh)}, device_id_type=MESH)

    lg_part[...] = jnp.zeros_like(lg_part)

    def logit_block(b, carry):
        at = pl.ds(pl.multiple_of(b * LANES, LANES), LANES)
        inner = dot_nt(ik_ref[...], iq_ref[at, :])
        inner_buf[b] = inner
        across = jnp.where(spread((queries, LANES), 0, jl, b * LANES), 1.0, 0.0).astype(BF16)
        weights = sum(dot(term, across) for term in terms(wt_ref[...]))
        head = lax.rem(iota((jl, LANES), 1), jl)
        weights = jnp.where(head == iota((jl, LANES), 0), weights, 0.0)
        weights = jnp.sum(weights, axis=0, keepdims=True)
        w_ref[pl.ds(b, 1), :] = weights
        p = jnp.maximum(inner, 0.0) * weights
        pick = jnp.where(spread((LANES, queries), 1, jl, b * LANES), 1.0, 0.0).astype(BF16)
        lg_part[...] += dot(jnp.concatenate(terms(p), axis=1), jnp.concatenate([pick] * 3, axis=0))
        return carry

    lax.fori_loop(0, jblocks, logit_block, 0)
    ikt[...] = ik_ref[...].astype(F32).T.astype(BF16)
    lat_ref[...] = latt_ref[...].T
    limit = jnp.concatenate([pos_ref[...] - base] * pair, axis=1)

    pl.semaphore_wait(barrier, nc - 1 + nh - 1)

    def head_rows(ref):
        return lambda d: ref.at[pl.ds(pl.multiple_of(d * share, share), share), :]

    pending = []
    lg_copies = start_all("head", nh, h, head_rows(lg_part), lambda o: lg_recv.at[o], lg_s, lg_r)
    pending += lg_copies
    load_q.wait()

    def scores(b, out):
        q = jnp.concatenate([q_buf[b * pair + p] for p in range(pair)], axis=1)
        s = dot(lat_ref[...], q)
        s = jnp.where(iota(s.shape, 0) <= limit, s, MASKED)
        out[...] = s
        return jnp.maximum(jnp.max(s, axis=0, keepdims=True), FLOOR)

    def exponentials(k, i, src, m):
        e = jnp.exp2((src[...] - m) * scale2)
        e_buf[k * GROUP + i] = e.astype(BF16)
        mst[k, pl.ds(i, 1), :] = m
        mst[k, pl.ds(GROUP + i, 1), :] = jnp.sum(e, axis=0, keepdims=True)

    def score_chunk(k, m):
        def score_pair(j, m):
            b = k * GROUP + 2 * j
            m_odd = scores(b + 1, s_odd)
            exponentials(k, 2 * j, s_even, m)
            m_even = scores(lax.rem(b + 2, blocks), s_even)
            exponentials(k, 2 * j + 1, s_odd, m_odd)
            return m_even

        m = lax.fori_loop(0, GROUP // 2, score_pair, m)
        return m, score_send(k)

    def score_send(k):
        return start_all(
            "ctx", nc, c, lambda d: mst.at[k], lambda o: mst_recv.at[k, o], mst_s.at[k], mst_r.at[k]
        )

    def logit_stats():
        for copy in lg_copies:
            copy.wait_recv()
        total = lg_part[own, :]
        for o in range(1, nh):
            total = total + lg_recv[o]
        total = jnp.where(iota(total.shape, 0) <= pos_ref[...] - own_base, total, MASKED)
        lgq[...] = total
        m = jnp.maximum(jnp.max(total, axis=0, keepdims=True), FLOOR)
        lsh[0:1, :] = m
        lsh[1:2, :] = jnp.sum(jnp.exp2((total - m) * LOG2E), axis=0, keepdims=True)
        return start_all("head", nh, h, lambda d: lsh, lambda o: lsh_recv.at[o], lsh_s, lsh_r)

    def combine(mine, others):
        m = mine[0:1, :]
        for other in others:
            m = jnp.maximum(m, other[0:1, :])
        total = mine[1:2, :] * jnp.exp2((mine[0:1, :] - m) * LOG2E)
        for other in others:
            total = total + other[1:2, :] * jnp.exp2((other[0:1, :] - m) * LOG2E)
        return m, total

    def logit_stats_ctx(copies):
        for copy in copies:
            copy.wait_recv()
        m, total = combine(lsh[...], [lsh_recv[o] for o in range(1, nh)])
        lsc[0:1, :] = m
        lsc[1:2, :] = total
        return start_all("ctx", nc, c, lambda d: lsc, lambda o: lsc_recv.at[o], lsc_s, lsc_r)

    lsh[...] = jnp.zeros_like(lsh)
    lsc[...] = jnp.zeros_like(lsc)
    mst_copies = []
    high = scores(0, s_even)
    for k in range(chunks):
        high, copies = score_chunk(k, high)
        mst_copies.append(copies)
    lsh_copies = logit_stats()
    pending += lsh_copies
    for copies in mst_copies:
        pending += copies

    t_acc[...] = jnp.zeros_like(t_acc)
    same = lax.rem(iota((queries, LANES), 1), queries) == iota((queries, LANES), 0)
    for k in range(chunks):
        for copy in mst_copies[k]:
            copy.wait_recv()
        mine = mst[k]
        highest = mine[:GROUP]
        for o in range(1, nc):
            highest = jnp.maximum(highest, mst_recv[k, o, :GROUP, :])
        shift = jnp.exp2((mine[:GROUP] - highest) * scale2)
        total = mine[GROUP:] * shift
        for o in range(1, nc):
            total = total + mst_recv[k, o, GROUP:, :] * jnp.exp2(
                (mst_recv[k, o, :GROUP, :] - highest) * scale2
            )
        factor = shift / total
        for i in range(GROUP):
            b = k * GROUP + i
            full = jnp.where(same, factor[i : i + 1, :], 0.0)
            hi = full.astype(BF16)
            low = (full - hi.astype(F32)).astype(BF16)
            t_acc[...] += dot_nt(e_buf[b], jnp.concatenate([hi, low], axis=0))
        if k == (chunks - 1) // 2:
            lsc_copies = logit_stats_ctx(lsh_copies)
            pending += lsc_copies
    t_part[...] = t_acc[:, :queries] + t_acc[:, queries:]
    tg_send[...] = t_part[...].astype(BF16)
    tg_copies = start_all("head", nh, h, head_rows(tg_send), lambda o: tg_recv.at[o], tg_s, tg_r)
    pending += tg_copies

    for copy in lsc_copies:
        copy.wait_recv()
    high, total = combine(lsc[...], [lsc_recv[o] for o in range(1, nc)])
    logits = lgq[...]
    predicted = jnp.exp2((logits - high) * LOG2E) * (1.0 / total)
    for copy in tg_copies:
        copy.wait_recv()
    target = t_part[own, :]
    for o in range(1, nh):
        target = target + tg_recv[o].astype(F32)
    gradient = jnp.where(
        iota(target.shape, 0) <= pos_ref[...] - own_base,
        math.sqrt(rows * nc) * (predicted - target * (1.0 / HEADS)),
        0.0,
    )
    gr_all[own, :] = gradient.astype(BF16)
    gr_copies = start_all("head", nh, h, lambda d: gr_all.at[own, :], lambda o: gr_all.at[own, :], gr_s, gr_r)
    pending += gr_copies
    for copy in gr_copies:
        copy.wait_recv()

    gk_acc[...] = jnp.zeros_like(gk_acc)

    def grad_block(b):
        at = pl.ds(pl.multiple_of(b * LANES, LANES), LANES)
        pick = jnp.where(spread((queries, LANES), 0, jl, b * LANES), 1.0, 0.0).astype(BF16)
        grad = dot(gr_all[...], pick)
        inner = inner_buf[b]
        gw_send[pl.ds(b, 1), :] = jnp.sum(grad * jnp.maximum(inner, 0.0), axis=0, keepdims=True)
        delta = jnp.where(inner > 0, grad * w_ref[pl.ds(b, 1), :], 0.0).astype(BF16)
        gk_acc[...] += dot(delta, iq_ref[at, :])
        block = dot(ikt[...], delta).T
        gq_f[at, :] = block
        gq_send[at, :] = block.astype(BF16)

    def gq_rows(dest):
        return pl.ds(pl.multiple_of(dest * drows, drows), drows)

    def pair_copy(o):
        dest = lax.rem(c // 2 + o, half) * 2 + 1 - lax.rem(c, 2)
        return pltpu.make_async_remote_copy(
            src_ref=gq_send.at[gq_rows(dest), :],
            dst_ref=pair_recv.at[o],
            send_sem=pair_s.at[o],
            recv_sem=pair_r.at[o],
            device_id={"ctx": c + 1 - 2 * lax.rem(c, 2)},
            device_id_type=MESH,
        )

    def gq_copy(o):
        dest = lax.rem(c // 2 + o, half) * 2 + lax.rem(c, 2)
        return pltpu.make_async_remote_copy(
            src_ref=gq_sum.at[o],
            dst_ref=gq_recv.at[o],
            send_sem=gq_s.at[o],
            recv_sem=gq_r.at[o],
            device_id={"ctx": dest},
            device_id_type=MESH,
        )

    half = nc // 2
    low = lax.rem(c, 2)
    if jblocks == nc:
        def grad_away(i, carry):
            o = lax.rem(i + 1, half)
            grad_block(lax.rem(c // 2 + o, half) * 2 + 1 - low)
            pair_copy(o).start()
            return carry

        def grad_near(i, carry):
            grad_block(lax.rem(c // 2 + i + 1, half) * 2 + low)
            return carry

        lax.fori_loop(0, half, grad_away, 0)
        lax.fori_loop(0, half, grad_near, 0)
    else:
        def grad_step(b, carry):
            grad_block(b)
            return carry

        lax.fori_loop(0, jblocks, grad_step, 0)
        for i in range(half):
            pair_copy((i + 1) % half).start()
    gk_send[...] = gk_acc[...].astype(BF16)
    gk_copies = start_all("head", nh, h, head_rows(gk_send), lambda o: gk_recv.at[o], gk_s, gk_r)
    gw_copies = start_all("ctx", nc, c, lambda d: gw_send, lambda o: gw_recv.at[o], gw_s, gw_r)
    pair_copies = [pair_copy(o) for o in range(half)]
    gq_copies = [gq_copy(o) for o in range(1, half)]

    def pair_sum(o):
        pair_copies[o].wait_recv()
        dest = lax.rem(c // 2 + o, half) * 2 + low
        return gq_f[gq_rows(dest), :] + pair_recv[o].astype(F32)

    for o in range(1, half):
        gq_sum[o] = pair_sum(o).astype(BF16)
        gq_copies[o - 1].start()
    pending += pair_copies
    pending += gk_copies + gw_copies + gq_copies

    for copy in gk_copies:
        copy.wait_recv()
    total = gk_acc[own, :]
    for o in range(1, nh):
        total = total + gk_recv[o].astype(F32)
    gk_out[...] = total
    total = pair_sum(0)
    for o in range(1, half):
        gq_copies[o - 1].wait_recv()
        total = total + gq_recv[o].astype(F32)
    gq_out[...] = total
    for copy in gw_copies:
        copy.wait_recv()
    total = gw_send[...]
    for o in range(1, nc):
        total = total + gw_recv[o]
    picked = jnp.zeros((queries // nc, LANES), F32)
    for b in range(jblocks):
        mine = spread(picked.shape, 0, jl, b * LANES - c * drows)
        picked = picked + jnp.where(mine, total[b : b + 1, :], 0.0)
    head = lax.rem(iota((LANES, jl), 0), jl) == iota((LANES, jl), 1)
    head = jnp.where(head, 1.0, 0.0).astype(BF16)
    gw_out[...] = sum(dot(term, head) for term in terms(picked))
    for copy in pending:
        copy.wait_send()


def finish(a_ref, b_ref, c_ref, a_out, b_out, c_out):
    a_out[...] = a_ref[...]
    b_out[...] = b_ref[...]
    c_out[...] = c_ref[...]


def local(nc, nh, positions, mla_queries, latent_keys, index_queries, index_keys, head_weights):
    queries, hl, dqk = mla_queries.shape
    _, jl, di = index_queries.shape
    rows = latent_keys.shape[0]
    share = rows // nh
    blocks = queries * hl // LANES
    jblocks = queries * jl // LANES
    chunks = blocks // GROUP
    own = queries // nc
    drows = own * jl
    q = mla_queries.transpose(1, 2, 0)
    iq = index_queries.reshape(queries * jl, di)
    vm = pltpu.VMEM
    dma = pltpu.SemaphoreType.DMA
    vspec = pl.BlockSpec(memory_space=pltpu.VMEM)
    gq, gk, gw = pl.pallas_call(
        functools.partial(kernel, nc, nh, hl, jl, queries),
        out_shape=(
            jax.ShapeDtypeStruct((drows, di), F32),
            jax.ShapeDtypeStruct((share, di), F32),
            jax.ShapeDtypeStruct((own, jl), F32),
        ),
        in_specs=[pl.BlockSpec(memory_space=pl.ANY)] + [vspec] * 5,
        out_specs=(vspec, vspec, vspec),
        scratch_shapes=[
            vm((hl, dqk, queries), BF16),
            vm((blocks, rows, LANES), BF16),
            vm((jblocks, rows, LANES), F32),
            vm((rows, queries), F32),
            vm((nh, share, queries), F32),
            vm((share, queries), F32),
            vm((8, queries), F32),
            vm((nh, 8, queries), F32),
            vm((8, queries), F32),
            vm((nc, 8, queries), F32),
            vm((chunks, 2 * GROUP, LANES), F32),
            vm((chunks, nc, 2 * GROUP, LANES), F32),
            vm((rows, 2 * queries), F32),
            vm((rows, queries), F32),
            vm((rows, queries), BF16),
            vm((nh, share, queries), BF16),
            vm((rows, queries), BF16),
            vm((rows, di), F32),
            vm((rows, di), BF16),
            vm((nh, share, di), BF16),
            vm((queries * jl, di), F32),
            vm((queries * jl, di), BF16),
            vm((nc // 2, drows, di), BF16),
            vm((jblocks, LANES), F32),
            vm((nc, jblocks, LANES), F32),
            vm((di, rows), BF16),
            vm((rows, dqk), BF16),
            vm((jblocks, LANES), F32),
            vm((rows, LANES), F32),
            vm((rows, LANES), F32),
            vm((nc // 2, drows, di), BF16),
            vm((nc // 2, drows, di), BF16),
            dma,
            dma((nh,)), dma((nh,)),
            dma((nh,)), dma((nh,)),
            dma((nc,)), dma((nc,)),
            dma((chunks, nc)), dma((chunks, nc)),
            dma((nh,)), dma((nh,)),
            dma((nh,)), dma((nh,)),
            dma((nh,)), dma((nh,)),
            dma((nc,)), dma((nc,)),
            dma((nc,)), dma((nc,)),
            dma((nc // 2,)), dma((nc // 2,)),
        ],
        compiler_params=pltpu.CompilerParams(
            collective_id=0, has_side_effects=True, vmem_limit_bytes=60 * 1024 * 1024
        ),
    )(q, latent_keys.T, iq, index_keys, head_weights.T, positions.reshape(1, queries))
    gq, gk, gw = pl.pallas_call(
        finish,
        out_shape=tuple(jax.ShapeDtypeStruct(x.shape, F32) for x in (gq, gk, gw)),
        in_specs=[vspec] * 3,
        out_specs=(vspec,) * 3,
    )(gq, gk, gw)
    return gq.reshape(own, jl, di), gk, gw


def solution(mesh):
    in_specs = (
        P(),
        P(None, "head", None),
        P("ctx", None),
        P(None, "head", None),
        P("ctx", None),
        P(None, "head"),
    )
    out_specs = (P("ctx", "head", None), P(("ctx", "head"), None), P("ctx", "head"))
    body = functools.partial(local, mesh.shape["ctx"], mesh.shape["head"])
    return jax.shard_map(body, mesh=mesh, in_specs=in_specs, out_specs=out_specs, check_vma=False)
```

```python
import functools
import math

import jax
import jax.numpy as jnp
from jax import lax
from jax.experimental import pallas as pl
from jax.experimental.pallas import tpu as pltpu
from jax.sharding import PartitionSpec as P

HEADS = 128
QK_HEAD = 192
LANES = 256
GROUP = 4
MESH = pl.DeviceIdType.MESH
F32 = jnp.float32
BF16 = jnp.bfloat16
MASKED = -1e30
FLOOR = -1e20
LOG2E = math.log2(math.e)
NT = (((1,), (1,)), ((), ()))


def dot(a, b):
    return jnp.dot(a, b, preferred_element_type=F32)


def dot_nt(a, b):
    return lax.dot_general(a, b, NT, preferred_element_type=F32)


def iota(shape, dim):
    return lax.broadcasted_iota(jnp.int32, shape, dim)


def spread(shape, query_dim, width, first):
    query = iota(shape, query_dim) * width
    lane = iota(shape, 1 - query_dim) + first
    return (query <= lane) & (lane < query + width)


def terms(x):
    hi = x.astype(BF16)
    rest = x - hi.astype(F32)
    mid = rest.astype(BF16)
    return hi, mid, (rest - mid.astype(F32)).astype(BF16)


def start_all(axis, n, me, source, slot, send, recv):
    copies = []
    for o in range(1, n):
        dest = lax.rem(me + o, n)
        copy = pltpu.make_async_remote_copy(
            src_ref=source(dest),
            dst_ref=slot(o),
            send_sem=send.at[o],
            recv_sem=recv.at[o],
            device_id={axis: dest},
            device_id_type=MESH,
        )
        copy.start()
        copies.append(copy)
    return copies


def kernel(
    nc, nh, hl, jl, queries,
    q_hbm, latt_hbm, iq_ref, ik_ref, wt_ref, pos_ref,
    gq_out, gk_out, gw_out,
    q_buf, e_buf, inner_buf, lg_part, lg_recv, lgq,
    lsh, lsh_recv, lsc, lsc_recv, mst, mst_recv, t_acc, t_part, tg_send, tg_recv,
    gr_all, gk_acc, gk_send, gk_recv, gq_f, gq_send, gq_recv, gw_send, gw_recv, ikt, lat_ref, w_ref, s_even, s_odd, pair_recv, gq_sum, latt_ref, latt_sem,
    q_sem, lg_s, lg_r, lsh_s, lsh_r, lsc_s, lsc_r, mst_s, mst_r, tg_s, tg_r,
    gr_s, gr_r, gk_s, gk_r, gq_s, gq_r, gw_s, gw_r, pair_s, pair_r,
):
    rows = latt_ref.shape[1]
    share = rows // nh
    pair = LANES // queries
    blocks = queries * hl // LANES
    jblocks = queries * jl // LANES
    drows = queries * jl // nc
    chunks = blocks // GROUP
    c = lax.axis_index("ctx")
    h = lax.axis_index("head")
    scale2 = LOG2E / math.sqrt(QK_HEAD)
    own = pl.ds(pl.multiple_of(h * share, share), share)
    base = c * rows
    own_base = base + h * share

    load_q = pltpu.make_async_copy(q_hbm, q_buf, q_sem)
    load_lat = pltpu.make_async_copy(latt_hbm, latt_ref, latt_sem)
    load_lat.start()
    load_q.start()

    barrier = pltpu.get_barrier_semaphore()
    for o in range(1, nc):
        pl.semaphore_signal(barrier, inc=1, device_id={"ctx": lax.rem(c + o, nc)}, device_id_type=MESH)
    for o in range(1, nh):
        pl.semaphore_signal(barrier, inc=1, device_id={"head": lax.rem(h + o, nh)}, device_id_type=MESH)

    lg_part[...] = jnp.zeros_like(lg_part)

    def logit_block(b, carry):
        at = pl.ds(pl.multiple_of(b * LANES, LANES), LANES)
        inner = dot_nt(ik_ref[...], iq_ref[at, :])
        inner_buf[b] = inner
        across = jnp.where(spread((queries, LANES), 0, jl, b * LANES), 1.0, 0.0).astype(BF16)
        weights = sum(dot(term, across) for term in terms(wt_ref[...]))
        head = lax.rem(iota((jl, LANES), 1), jl)
        weights = jnp.where(head == iota((jl, LANES), 0), weights, 0.0)
        weights = jnp.sum(weights, axis=0, keepdims=True)
        w_ref[pl.ds(b, 1), :] = weights
        p = jnp.maximum(inner, 0.0) * weights
        pick = jnp.where(spread((LANES, queries), 1, jl, b * LANES), 1.0, 0.0).astype(BF16)
        lg_part[...] += dot(jnp.concatenate(terms(p), axis=1), jnp.concatenate([pick] * 3, axis=0))
        return carry

    lax.fori_loop(0, jblocks, logit_block, 0)
    limit = jnp.concatenate([pos_ref[...] - base] * pair, axis=1)

    pl.semaphore_wait(barrier, nc - 1 + nh - 1)

    def head_rows(ref):
        return lambda d: ref.at[pl.ds(pl.multiple_of(d * share, share), share), :]

    pending = []
    lg_copies = start_all("head", nh, h, head_rows(lg_part), lambda o: lg_recv.at[o], lg_s, lg_r)
    pending += lg_copies
    load_lat.wait()
    lat_ref[...] = latt_ref[...].T
    ikt[...] = ik_ref[...].astype(F32).T.astype(BF16)
    load_q.wait()

    def scores(b, out):
        q = jnp.concatenate([q_buf[b * pair + p] for p in range(pair)], axis=1)
        s = dot(lat_ref[...], q)
        s = jnp.where(iota(s.shape, 0) <= limit, s, MASKED)
        out[...] = s
        return jnp.maximum(jnp.max(s, axis=0, keepdims=True), FLOOR)

    def exponentials(k, i, src, m):
        e = jnp.exp2((src[...] - m) * scale2)
        e_buf[k * GROUP + i] = e.astype(BF16)
        mst[k, pl.ds(i, 1), :] = m
        mst[k, pl.ds(GROUP + i, 1), :] = jnp.sum(e, axis=0, keepdims=True)

    def score_chunk(k, m):
        def score_pair(j, m):
            b = k * GROUP + 2 * j
            m_odd = scores(b + 1, s_odd)
            exponentials(k, 2 * j, s_even, m)
            m_even = scores(lax.rem(b + 2, blocks), s_even)
            exponentials(k, 2 * j + 1, s_odd, m_odd)
            return m_even

        m = lax.fori_loop(0, GROUP // 2, score_pair, m)
        return m, score_send(k)

    def score_send(k):
        return start_all(
            "ctx", nc, c, lambda d: mst.at[k], lambda o: mst_recv.at[k, o], mst_s.at[k], mst_r.at[k]
        )

    def logit_stats():
        for copy in lg_copies:
            copy.wait_recv()
        total = lg_part[own, :]
        for o in range(1, nh):
            total = total + lg_recv[o]
        total = jnp.where(iota(total.shape, 0) <= pos_ref[...] - own_base, total, MASKED)
        lgq[...] = total
        m = jnp.maximum(jnp.max(total, axis=0, keepdims=True), FLOOR)
        lsh[0:1, :] = m
        lsh[1:2, :] = jnp.sum(jnp.exp2((total - m) * LOG2E), axis=0, keepdims=True)
        return start_all("head", nh, h, lambda d: lsh, lambda o: lsh_recv.at[o], lsh_s, lsh_r)

    def combine(mine, others):
        m = mine[0:1, :]
        for other in others:
            m = jnp.maximum(m, other[0:1, :])
        total = mine[1:2, :] * jnp.exp2((mine[0:1, :] - m) * LOG2E)
        for other in others:
            total = total + other[1:2, :] * jnp.exp2((other[0:1, :] - m) * LOG2E)
        return m, total

    def logit_stats_ctx(copies):
        for copy in copies:
            copy.wait_recv()
        m, total = combine(lsh[...], [lsh_recv[o] for o in range(1, nh)])
        lsc[0:1, :] = m
        lsc[1:2, :] = total
        return start_all("ctx", nc, c, lambda d: lsc, lambda o: lsc_recv.at[o], lsc_s, lsc_r)

    lsh[...] = jnp.zeros_like(lsh)
    lsc[...] = jnp.zeros_like(lsc)
    mst_copies = []
    high = scores(0, s_even)
    for k in range(chunks):
        high, copies = score_chunk(k, high)
        mst_copies.append(copies)
    lsh_copies = logit_stats()
    pending += lsh_copies
    for copies in mst_copies:
        pending += copies

    t_acc[...] = jnp.zeros_like(t_acc)
    same = lax.rem(iota((queries, LANES), 1), queries) == iota((queries, LANES), 0)
    for k in range(chunks):
        for copy in mst_copies[k]:
            copy.wait_recv()
        mine = mst[k]
        highest = mine[:GROUP]
        for o in range(1, nc):
            highest = jnp.maximum(highest, mst_recv[k, o, :GROUP, :])
        shift = jnp.exp2((mine[:GROUP] - highest) * scale2)
        total = mine[GROUP:] * shift
        for o in range(1, nc):
            total = total + mst_recv[k, o, GROUP:, :] * jnp.exp2(
                (mst_recv[k, o, :GROUP, :] - highest) * scale2
            )
        factor = shift / total
        for i in range(GROUP):
            b = k * GROUP + i
            full = jnp.where(same, factor[i : i + 1, :], 0.0)
            hi = full.astype(BF16)
            low = (full - hi.astype(F32)).astype(BF16)
            t_acc[...] += dot_nt(e_buf[b], jnp.concatenate([hi, low], axis=0))
        if k == (chunks - 1) // 2:
            lsc_copies = logit_stats_ctx(lsh_copies)
            pending += lsc_copies
    t_part[...] = t_acc[:, :queries] + t_acc[:, queries:]
    tg_send[...] = t_part[...].astype(BF16)
    tg_copies = start_all("head", nh, h, head_rows(tg_send), lambda o: tg_recv.at[o], tg_s, tg_r)
    pending += tg_copies

    for copy in lsc_copies:
        copy.wait_recv()
    high, total = combine(lsc[...], [lsc_recv[o] for o in range(1, nc)])
    logits = lgq[...]
    predicted = jnp.exp2((logits - high) * LOG2E) * (1.0 / total)
    for copy in tg_copies:
        copy.wait_recv()
    target = t_part[own, :]
    for o in range(1, nh):
        target = target + tg_recv[o].astype(F32)
    gradient = jnp.where(
        iota(target.shape, 0) <= pos_ref[...] - own_base,
        math.sqrt(rows * nc) * (predicted - target * (1.0 / HEADS)),
        0.0,
    )
    gr_all[own, :] = gradient.astype(BF16)
    gr_copies = start_all("head", nh, h, lambda d: gr_all.at[own, :], lambda o: gr_all.at[own, :], gr_s, gr_r)
    pending += gr_copies
    for copy in gr_copies:
        copy.wait_recv()

    gk_acc[...] = jnp.zeros_like(gk_acc)

    def grad_block(b):
        at = pl.ds(pl.multiple_of(b * LANES, LANES), LANES)
        pick = jnp.where(spread((queries, LANES), 0, jl, b * LANES), 1.0, 0.0).astype(BF16)
        grad = dot(gr_all[...], pick)
        inner = inner_buf[b]
        gw_send[pl.ds(b, 1), :] = jnp.sum(grad * jnp.maximum(inner, 0.0), axis=0, keepdims=True)
        delta = jnp.where(inner > 0, grad * w_ref[pl.ds(b, 1), :], 0.0).astype(BF16)
        gk_acc[...] += dot(delta, iq_ref[at, :])
        block = dot(ikt[...], delta).T
        gq_f[at, :] = block
        gq_send[at, :] = block.astype(BF16)

    def gq_rows(dest):
        return pl.ds(pl.multiple_of(dest * drows, drows), drows)

    def pair_copy(o):
        dest = lax.rem(c // 2 + o, half) * 2 + 1 - lax.rem(c, 2)
        return pltpu.make_async_remote_copy(
            src_ref=gq_send.at[gq_rows(dest), :],
            dst_ref=pair_recv.at[o],
            send_sem=pair_s.at[o],
            recv_sem=pair_r.at[o],
            device_id={"ctx": c + 1 - 2 * lax.rem(c, 2)},
            device_id_type=MESH,
        )

    def gq_copy(o):
        dest = lax.rem(c // 2 + o, half) * 2 + lax.rem(c, 2)
        return pltpu.make_async_remote_copy(
            src_ref=gq_sum.at[o],
            dst_ref=gq_recv.at[o],
            send_sem=gq_s.at[o],
            recv_sem=gq_r.at[o],
            device_id={"ctx": dest},
            device_id_type=MESH,
        )

    half = nc // 2
    low = lax.rem(c, 2)
    if jblocks == nc:
        def grad_away(i, carry):
            o = lax.rem(i + 1, half)
            grad_block(lax.rem(c // 2 + o, half) * 2 + 1 - low)
            pair_copy(o).start()
            return carry

        def grad_near(i, carry):
            grad_block(lax.rem(c // 2 + i + 1, half) * 2 + low)
            return carry

        lax.fori_loop(0, half, grad_away, 0)
        lax.fori_loop(0, half, grad_near, 0)
    else:
        def grad_step(b, carry):
            grad_block(b)
            return carry

        lax.fori_loop(0, jblocks, grad_step, 0)
        for i in range(half):
            pair_copy((i + 1) % half).start()
    gk_send[...] = gk_acc[...].astype(BF16)
    gk_copies = start_all("head", nh, h, head_rows(gk_send), lambda o: gk_recv.at[o], gk_s, gk_r)
    gw_copies = start_all("ctx", nc, c, lambda d: gw_send, lambda o: gw_recv.at[o], gw_s, gw_r)
    pair_copies = [pair_copy(o) for o in range(half)]
    gq_copies = [gq_copy(o) for o in range(1, half)]

    def pair_sum(o):
        pair_copies[o].wait_recv()
        dest = lax.rem(c // 2 + o, half) * 2 + low
        return gq_f[gq_rows(dest), :] + pair_recv[o].astype(F32)

    for o in range(1, half):
        gq_sum[o] = pair_sum(o).astype(BF16)
        gq_copies[o - 1].start()
    pending += pair_copies
    pending += gk_copies + gw_copies + gq_copies

    for copy in gk_copies:
        copy.wait_recv()
    total = gk_acc[own, :]
    for o in range(1, nh):
        total = total + gk_recv[o].astype(F32)
    gk_out[...] = total
    total = pair_sum(0)
    for o in range(1, half):
        gq_copies[o - 1].wait_recv()
        total = total + gq_recv[o].astype(F32)
    gq_out[...] = total
    for copy in gw_copies:
        copy.wait_recv()
    total = gw_send[...]
    for o in range(1, nc):
        total = total + gw_recv[o]
    picked = jnp.zeros((queries // nc, LANES), F32)
    for b in range(jblocks):
        mine = spread(picked.shape, 0, jl, b * LANES - c * drows)
        picked = picked + jnp.where(mine, total[b : b + 1, :], 0.0)
    head = lax.rem(iota((LANES, jl), 0), jl) == iota((LANES, jl), 1)
    head = jnp.where(head, 1.0, 0.0).astype(BF16)
    gw_out[...] = sum(dot(term, head) for term in terms(picked))
    for copy in pending:
        copy.wait_send()


def finish(a_ref, b_ref, c_ref, a_out, b_out, c_out):
    a_out[...] = a_ref[...]
    b_out[...] = b_ref[...]
    c_out[...] = c_ref[...]


def local(nc, nh, positions, mla_queries, latent_keys, index_queries, index_keys, head_weights):
    queries, hl, dqk = mla_queries.shape
    _, jl, di = index_queries.shape
    rows = latent_keys.shape[0]
    share = rows // nh
    blocks = queries * hl // LANES
    jblocks = queries * jl // LANES
    chunks = blocks // GROUP
    own = queries // nc
    drows = own * jl
    q = mla_queries.transpose(1, 2, 0)
    iq = index_queries.reshape(queries * jl, di)
    vm = pltpu.VMEM
    dma = pltpu.SemaphoreType.DMA
    vspec = pl.BlockSpec(memory_space=pltpu.VMEM)
    gq, gk, gw = pl.pallas_call(
        functools.partial(kernel, nc, nh, hl, jl, queries),
        out_shape=(
            jax.ShapeDtypeStruct((drows, di), F32),
            jax.ShapeDtypeStruct((share, di), F32),
            jax.ShapeDtypeStruct((own, jl), F32),
        ),
        in_specs=[pl.BlockSpec(memory_space=pl.ANY)] * 2 + [vspec] * 4,
        out_specs=(vspec, vspec, vspec),
        scratch_shapes=[
            vm((hl, dqk, queries), BF16),
            vm((blocks, rows, LANES), BF16),
            vm((jblocks, rows, LANES), F32),
            vm((rows, queries), F32),
            vm((nh, share, queries), F32),
            vm((share, queries), F32),
            vm((8, queries), F32),
            vm((nh, 8, queries), F32),
            vm((8, queries), F32),
            vm((nc, 8, queries), F32),
            vm((chunks, 2 * GROUP, LANES), F32),
            vm((chunks, nc, 2 * GROUP, LANES), F32),
            vm((rows, 2 * queries), F32),
            vm((rows, queries), F32),
            vm((rows, queries), BF16),
            vm((nh, share, queries), BF16),
            vm((rows, queries), BF16),
            vm((rows, di), F32),
            vm((rows, di), BF16),
            vm((nh, share, di), BF16),
            vm((queries * jl, di), F32),
            vm((queries * jl, di), BF16),
            vm((nc // 2, drows, di), BF16),
            vm((jblocks, LANES), F32),
            vm((nc, jblocks, LANES), F32),
            vm((di, rows), BF16),
            vm((rows, dqk), BF16),
            vm((jblocks, LANES), F32),
            vm((rows, LANES), F32),
            vm((rows, LANES), F32),
            vm((nc // 2, drows, di), BF16),
            vm((nc // 2, drows, di), BF16),
            vm((dqk, rows), BF16),
            dma,
            dma,
            dma((nh,)), dma((nh,)),
            dma((nh,)), dma((nh,)),
            dma((nc,)), dma((nc,)),
            dma((chunks, nc)), dma((chunks, nc)),
            dma((nh,)), dma((nh,)),
            dma((nh,)), dma((nh,)),
            dma((nh,)), dma((nh,)),
            dma((nc,)), dma((nc,)),
            dma((nc,)), dma((nc,)),
            dma((nc // 2,)), dma((nc // 2,)),
        ],
        compiler_params=pltpu.CompilerParams(
            collective_id=0, has_side_effects=True, vmem_limit_bytes=60 * 1024 * 1024
        ),
    )(q, latent_keys.T, iq, index_keys, head_weights.T, positions.reshape(1, queries))
    gq, gk, gw = pl.pallas_call(
        finish,
        out_shape=tuple(jax.ShapeDtypeStruct(x.shape, F32) for x in (gq, gk, gw)),
        in_specs=[vspec] * 3,
        out_specs=(vspec,) * 3,
    )(gq, gk, gw)
    return gq.reshape(own, jl, di), gk, gw


def solution(mesh):
    in_specs = (
        P(),
        P(None, "head", None),
        P("ctx", None),
        P(None, "head", None),
        P("ctx", None),
        P(None, "head"),
    )
    out_specs = (P("ctx", "head", None), P(("ctx", "head"), None), P("ctx", "head"))
    body = functools.partial(local, mesh.shape["ctx"], mesh.shape["head"])
    return jax.shard_map(body, mesh=mesh, in_specs=in_specs, out_specs=out_specs, check_vma=False)
```
